32 devices in a mesh: views: 4 (over z), bricks: 8 (over y, x, core).
Axes of the slice: x: 2, y: 2, z: 4, core: 2. Of those that a mesh axis runs over, the one named last changes fastest.
Arguments:
- tile_pixel: int32 [4, 8, 32], P('views', 'bricks'), may hold values from 0 to 15
- tile_voxel: int32 [4, 8, 32], P('views', 'bricks'), may hold values from 0 to 63
- tile_count: int32 [4, 8], P('views', 'bricks'), may hold values from 8 to 32, as said below
- features: bfloat16 [4, 8, 16, 64, 128], P('views', 'bricks'), may hold values from -6 to 6
- interp: bfloat16 [4, 8, 32, 128, 512], P('views', 'bricks'), may hold values from -0.5 to 0.5
- conv_weight: bfloat16 [3, 3, 3, 64, 64], replicated, may hold values from -0.15625 to 0.15625
- conv_bias: float32 [64], replicated, may hold values from -3 to 3
- smooth_coef: float32 [64, 128, 128], P('bricks', 'views'), may hold values from 0.04 to 0.16
Outputs:
- volume: bfloat16 [64, 64, 128, 128], P(None, 'bricks', 'views')
The draws below stay inside these ranges and needn't reach their ends.
Inputs may be any that keep to these rules, and one draw needn't show every extreme that they name: `tile_count`: between 8 and 32 live tiles a device; counts are shared largely within a view group; some device has all 32 slots live in every draw.
All inputs are finite; a program needn't handle non-finite values.
Results may differ from the reference program's by a relative error of at most 0.0037.
Values may be sent and summed in bfloat16 or wider, within the bound.
A program may use at most 256 MiB of HBM per device.

```python
import math
import jax
import jax.numpy as jnp
from jax import lax

C = 64
PIX = 128
Z = 128
BX = 8
BY = 32
PIXB = 16
BLK_DEV = 64
VOXB = 512
X = 64
Y = 128
N_VIEWS = 4
N_BRICKS = 8
DEVICES = 32


def draw_tile_count(key, part):
    key_top = jax.random.fold_in(key, 11)
    key_drop = jax.random.fold_in(key, 12)
    key_pick = jax.random.fold_in(key, 13)
    lowest = DEVICES // 4
    view_top = jax.random.randint(key_top, (N_VIEWS, 1), lowest, DEVICES + 1)
    dropped = jax.random.randint(key_drop, (N_VIEWS, N_BRICKS), 0, DEVICES // 4 + 1)
    counts = jnp.maximum(view_top - dropped, lowest).reshape(-1)
    picked = jax.random.randint(key_pick, (), 0, N_VIEWS * N_BRICKS)
    counts = jnp.where(jnp.arange(N_VIEWS * N_BRICKS) == picked, DEVICES, counts)
    return counts.reshape(N_VIEWS, N_BRICKS).astype(jnp.int32)


def with_ends(array, rng, smallest, top_value):
    dims = array.shape
    spot = [jax.random.randint(jax.random.fold_in(rng, axis), (), 0, dims[axis]) for axis in range(len(dims))]
    array = array.at[tuple(spot)].set(smallest)
    longest = dims.index(max(dims))
    spot[longest] = (spot[longest] + 1) % dims[longest]
    return array.at[tuple(spot)].set(top_value)


def levels(rng, shape, cuts, low, top_value):
    gain, own = 1.0, jax.random.fold_in(rng, 6)
    for axis_at, shards_of in cuts:
        draws = jnp.exp(jax.random.uniform(jax.random.fold_in(own, axis_at), (shards_of,), jnp.float32, low / len(cuts), top_value / len(cuts)))
        gain = gain * jnp.repeat(draws, shape[axis_at] // shards_of).reshape([-1 if axis == axis_at else 1 for axis in range(len(shape))])
    return gain


def scatter_about(stream_key, dims, scale, most, cuts=(), kind=jnp.bfloat16):
    gain = levels(stream_key, dims, cuts, -0.22, 0.18) if cuts else 1.0
    values = jax.random.normal(stream_key, dims, jnp.float32) * scale * gain
    return jnp.minimum(jnp.maximum(values, -most), most).astype(kind)


def setup_inputs(seed: int = 0) -> dict:
    seeds = jax.random.split(jax.random.key(seed), 9)
    return {
        "tile_pixel": with_ends(jax.random.randint(seeds[0], (N_VIEWS, N_BRICKS, N_VIEWS * N_BRICKS), 0, PIXB), jax.random.fold_in(seeds[0], 1), 0, PIXB - 1).astype(jnp.int32),
        "tile_voxel": with_ends(jax.random.randint(seeds[1], (N_VIEWS, N_BRICKS, N_VIEWS * N_BRICKS), 0, BLK_DEV), jax.random.fold_in(seeds[1], 1), 0, BLK_DEV - 1).astype(jnp.int32),
        "tile_count": draw_tile_count(jax.random.fold_in(seeds[8], 71), 0),
        "features": scatter_about(seeds[3], (N_VIEWS, N_BRICKS, PIXB, C, PIX), 1.0, 6.0, ((0, 4), (1, 8))),
        "interp": scatter_about(seeds[4], (N_VIEWS, N_BRICKS, N_VIEWS * N_BRICKS, PIX, VOXB), PIX ** -0.5, 0.5, ((0, 4), (1, 8))),
        "conv_weight": scatter_about(seeds[5], (3, 3, 3, C, C), (27 * C) ** -0.5, 0.15625),
        "conv_bias": scatter_about(seeds[6], (C,), 0.5, 3.0, (), jnp.float32),
        "smooth_coef": jnp.clip(jnp.exp(math.log(0.16) - 1.3862944 * jax.random.uniform(seeds[7], (X, Y, Z), jnp.float32) ** levels(seeds[7], (X, Y, Z), ((0, 8), (1, 4)), -0.2, 0.2)), 0.04, 0.16),
    }


def lift_step(total, item):
    feats, tiles, pixel_ids, voxel_ids, count, sender = item
    slot_ids = jnp.arange(DEVICES, dtype=jnp.int32)
    offset = jnp.remainder(sender * 37, DEVICES)
    live = (jnp.remainder(slot_ids - offset, DEVICES) < count).astype(jnp.float32)
    chosen = feats[pixel_ids]
    part = jnp.einsum("dcp,dpv->dcv", chosen.astype(jnp.float32), tiles.astype(jnp.float32))
    rounded = lax.optimization_barrier(part.astype(jnp.bfloat16))
    part = rounded.astype(jnp.float32)
    total = total.at[slot_ids, voxel_ids].add(part * live[:, None, None])
    return total, None


def convolve_slab(stacked, weights, conv_bias, width_x, width_y):
    total = jnp.zeros((C, width_x, width_y, Z), jnp.float32)
    for shift_x in range(3):
        for shift_y in range(3):
            window = stacked[:, shift_x:shift_x + width_x, shift_y:shift_y + width_y, :]
            total = total + jnp.einsum("oi,ixyz->oxyz", weights[shift_x * 3 + shift_y].astype(jnp.float32), window.astype(jnp.float32))
    return jax.nn.relu(total + conv_bias[:, None, None, None])


def reference(tile_pixel, tile_voxel, tile_count, features, interp, conv_weight, conv_bias, smooth_coef):
    senders = jnp.arange(DEVICES, dtype=jnp.int32)
    items = (features.reshape(DEVICES, PIXB, C, PIX), interp.reshape(DEVICES, DEVICES, PIX, VOXB),
             tile_pixel.reshape(DEVICES, DEVICES), tile_voxel.reshape(DEVICES, DEVICES),
             tile_count.reshape(DEVICES), senders)
    start = jnp.zeros((DEVICES, BLK_DEV, C, VOXB), jnp.float32)
    blocks, unused = lax.scan(lift_step, start, items)
    blocks = blocks.reshape(N_VIEWS, N_BRICKS, BX, BY // 4, C, 4, Z)
    lifted = jnp.transpose(blocks, (4, 1, 2, 0, 3, 5, 6)).reshape(C, X, Y, Z)
    rectified = jax.nn.relu(lifted).astype(jnp.bfloat16)
    padded = jnp.pad(rectified, ((0, 0), (1, 1), (1, 1), (1, 1)))
    stacked = jnp.concatenate([padded[..., 0:Z], padded[..., 1:Z + 1], padded[..., 2:Z + 2]], axis=0)
    weights = jnp.transpose(conv_weight, (0, 1, 3, 2, 4)).reshape(9, C, 3 * C)

    def slab(index):
        piece = lax.dynamic_slice_in_dim(stacked, index * BX, BX + 2, 1)
        return convolve_slab(piece, weights, conv_bias, BX, Y)

    slabs = lax.map(slab, jnp.arange(N_BRICKS, dtype=jnp.int32))
    gated = jnp.transpose(slabs, (1, 0, 2, 3, 4)).reshape(C, X, Y, Z)
    beside_all = jnp.pad(gated, ((0, 0), (1, 1), (1, 1), (1, 1)))
    beside = beside_all[:, 2:, 1:-1, 1:-1] + beside_all[:, :-2, 1:-1, 1:-1]
    beside = beside + beside_all[:, 1:-1, 2:, 1:-1] + beside_all[:, 1:-1, :-2, 1:-1]
    beside = beside + beside_all[:, 1:-1, 1:-1, 2:] + beside_all[:, 1:-1, 1:-1, :-2]
    volume = gated + smooth_coef[None] * (beside - 6.0 * gated)
    return volume.astype(jnp.bfloat16)
```

```python
import functools

import jax
import jax.numpy as jnp
from jax import lax
from jax.experimental import pallas as pl
from jax.experimental.pallas import tpu as pltpu
from jax.sharding import PartitionSpec as P

MESH = pl.DeviceIdType.MESH
DIRS = ((0, 1), (0, -1), (1, 0), (-1, 0), (1, 1), (1, -1), (-1, 1), (-1, -1))
LIMIT = 60 * 1024 * 1024


def lift_kernel(group, pixel_ref, ids_ref, feats_ref, tiles_ref, out_ref):
    step = pl.program_id(0)
    channels = feats_ref.shape[1]
    lanes = out_ref.shape[2]
    parts = tiles_ref.shape[2] // lanes
    for k in range(group):
        slot = step * group + k
        chosen = feats_ref[pixel_ref[slot]]
        value = jnp.dot(chosen, tiles_ref[k], preferred_element_type=jnp.float32)
        value = value.astype(jnp.bfloat16)
        for part in range(parts):
            out_ref[k, part * channels : (part + 1) * channels, :] = value[
                :, part * lanes : (part + 1) * lanes
            ]
        tail = out_ref.shape[1] - parts * channels
        ident = jnp.full((tail, lanes), ids_ref[slot], jnp.int32)
        out_ref[k, parts * channels :, :] = ident.astype(jnp.float32).astype(jnp.bfloat16)


def lift(pixel_ids, ids, feats, tiles, depth):
    slots, pixels, voxels = tiles.shape
    channels = feats.shape[1]
    group = 4
    rows = voxels // depth * channels + 8
    return pl.pallas_call(
        functools.partial(lift_kernel, group),
        out_shape=jax.ShapeDtypeStruct((slots, rows, depth), jnp.bfloat16),
        grid_spec=pltpu.PrefetchScalarGridSpec(
            num_scalar_prefetch=2,
            grid=(slots // group,),
            in_specs=[
                pl.BlockSpec(feats.shape, lambda i, *_: (0, 0, 0)),
                pl.BlockSpec((group, pixels, voxels), lambda i, *_: (i, 0, 0)),
            ],
            out_specs=pl.BlockSpec((group, rows, depth), lambda i, *_: (i, 0, 0)),
        ),
        name="lift",
    )(pixel_ids, ids, feats, tiles)


def scatter_kernel(ids_ref, got_ref, out_ref, acc):
    slots = got_ref.shape[0]
    blocks = out_ref.shape[0]
    rows = out_ref.shape[1]

    def clear(i, _):
        acc[i] = jnp.zeros(acc.shape[1:], jnp.float32)
        return 0

    def add(d, _):
        i = ids_ref[d]
        acc[i] = acc[i] + got_ref[d, 0:rows, :].astype(jnp.float32)
        return 0

    def put(i, _):
        out_ref[i] = jnp.maximum(acc[i], 0.0).astype(jnp.bfloat16)
        return 0

    lax.fori_loop(0, blocks, clear, 0)
    lax.fori_loop(0, slots, add, 0)
    lax.fori_loop(0, blocks, put, 0)


def scatter(ids, got, blocks):
    rows = got.shape[1] - 8
    depth = got.shape[2]
    return pl.pallas_call(
        scatter_kernel,
        out_shape=jax.ShapeDtypeStruct((blocks, rows, depth), jnp.bfloat16),
        grid_spec=pltpu.PrefetchScalarGridSpec(
            num_scalar_prefetch=1,
            grid=(1,),
            in_specs=[pl.BlockSpec(got.shape, lambda i, *_: (0, 0, 0))],
            out_specs=pl.BlockSpec((blocks, rows, depth), lambda i, *_: (0, 0, 0)),
            scratch_shapes=[pltpu.VMEM((blocks + 1, rows, depth), jnp.float32)],
        ),
        compiler_params=pltpu.CompilerParams(vmem_limit_bytes=LIMIT),
        name="scatter",
    )(ids, got)


def conv_kernel(
    views, bricks, r_ref, w_ref, bias_ref, coef_ref, out_ref,
    padded, stack, prod, gated, obuf, own_sem, send_sem, recv_sem, out_sem,
):
    v = lax.axis_index("views")
    b = lax.axis_index("bricks")
    size_x, size_y, ch, depth = r_ref.shape
    wide = 3 * ch

    def there(dv, db):
        return (v + dv >= 0) & (v + dv < views) & (b + db >= 0) & (b + db < bricks)

    def count(dv, db):
        return jnp.where(there(dv, db), 1, 0)

    own = pltpu.make_async_copy(
        r_ref, padded.at[pl.ds(2, size_x), pl.ds(2, size_y)], own_sem
    )
    own.start()

    barrier = pltpu.get_barrier_semaphore()
    total = 0
    for dv, db in DIRS:
        total = total + count(dv, db)

        @pl.when(there(dv, db))
        def _(dv=dv, db=db):
            pl.semaphore_signal(barrier, inc=1, device_id=(v + dv, b + db), device_id_type=MESH)

    pl.semaphore_wait(barrier, total)

    def span(delta, size):
        if delta == 0:
            return pl.ds(0, size), pl.ds(2, size)
        if delta == 1:
            return pl.ds(size - 2, 2), pl.ds(0, 2)
        return pl.ds(0, 2), pl.ds(size + 2, 2)

    def copy(k):
        dv, db = DIRS[k]
        from_x, to_x = span(db, size_x)
        from_y, to_y = span(dv, size_y)
        return pltpu.make_async_remote_copy(
            src_ref=r_ref.at[from_x, from_y],
            dst_ref=padded.at[to_x, to_y],
            send_sem=send_sem.at[k],
            recv_sem=recv_sem.at[k],
            device_id=(v + dv, b + db),
            device_id_type=MESH,
        )

    for k in range(len(DIRS)):
        dv, db = DIRS[k]

        @pl.when(there(dv, db))
        def _(k=k):
            copy(k).start()

    def receive(k):
        dv, db = DIRS[k]
        _, to_x = span(db, size_x)
        _, to_y = span(dv, size_y)

        @pl.when(there(-dv, -db))
        def _():
            copy(k).wait_recv()

        @pl.when(jnp.logical_not(there(-dv, -db)))
        def _():
            view = padded.at[to_x, to_y]
            view[...] = jnp.zeros(view.shape, jnp.bfloat16)

    def stack_plane(p):
        lane = lax.broadcasted_iota(jnp.int32, (ch, depth), 1)

        def row(y, _):
            at = pl.ds(pl.multiple_of(y * depth, depth), depth)
            here = padded[p, y]
            wide_here = here.astype(jnp.float32)
            before = jnp.where(lane == 0, 0.0, pltpu.roll(wide_here, 1, 1))
            after = jnp.where(lane == depth - 1, 0.0, pltpu.roll(wide_here, depth - 1, 1))
            base = p * wide
            stack[pl.ds(pl.multiple_of(base, ch), ch), at] = before.astype(jnp.bfloat16)
            stack[pl.ds(pl.multiple_of(base + ch, ch), ch), at] = here
            stack[pl.ds(pl.multiple_of(base + 2 * ch, ch), ch), at] = after.astype(jnp.bfloat16)
            return 0

        lax.fori_loop(0, size_y + 4, row, 0, unroll=4)

    lanes = 4 * depth
    chunks = (size_y + 4) // 4

    def conv_plane(g):
        rows = pl.ds(pl.multiple_of(g * wide, ch), 3 * wide)

        def chunk(c, _):
            at = pl.ds(pl.multiple_of(c * lanes, lanes), lanes)
            prod[:, at] = jnp.dot(w_ref[...], stack[rows, at], preferred_element_type=jnp.float32)
            return 0

        lax.fori_loop(0, chunks, chunk, 0, unroll=3)
        x = b * size_x + g - 1
        x_fits = (x >= 0) & (x < bricks * size_x)

        def row(y, _):
            at0 = pl.ds(pl.multiple_of(y * depth, depth), depth)
            at1 = pl.ds(pl.multiple_of((y + 1) * depth, depth), depth)
            at2 = pl.ds(pl.multiple_of((y + 2) * depth, depth), depth)
            value = prod[0:ch, at0] + prod[ch : 2 * ch, at1] + prod[2 * ch : wide, at2]
            value = jnp.maximum(value + bias_ref[...], 0.0)
            y_all = v * size_y + y - 1
            fits = x_fits & (y_all >= 0) & (y_all < views * size_y)
            gated[g, y] = value * jnp.where(fits, 1.0, 0.0)
            return 0

        lax.fori_loop(0, size_y + 2, row, 0, unroll=2)

    def loop(low, high, body):
        def step(i, _):
            body(i)
            return 0

        lax.fori_loop(low, high, step, 0)

    own.wait()
    receive(2)
    receive(3)
    loop(2, size_x + 2, stack_plane)
    loop(2, size_x, conv_plane)
    for k in (0, 1, 4, 5, 6, 7):
        receive(k)
    loop(0, 2, stack_plane)
    loop(size_x + 2, size_x + 4, stack_plane)
    loop(0, 2, conv_plane)
    loop(size_x, size_x + 2, conv_plane)

    def smooth_plane(x):
        lane = lax.broadcasted_iota(jnp.int32, (ch, depth), 1)

        def row(y, _):
            here = gated[x + 1, y + 1]
            beside = gated[x, y + 1] + gated[x + 2, y + 1] + gated[x + 1, y] + gated[x + 1, y + 2]
            before = jnp.where(lane == 0, 0.0, pltpu.roll(here, 1, 1))
            after = jnp.where(lane == depth - 1, 0.0, pltpu.roll(here, depth - 1, 1))
            beside = beside + before + after
            coef = coef_ref[x, pl.ds(y, 1), :]
            obuf[x, y] = (here + coef * (beside - 6.0 * here)).astype(jnp.bfloat16)
            return 0

        lax.fori_loop(0, size_y, row, 0, unroll=2)

    for x in range(size_x):
        smooth_plane(x)
        pltpu.make_async_copy(obuf.at[x], out_ref.at[x], out_sem.at[x]).start()
    for x in range(size_x):
        pltpu.make_async_copy(obuf.at[x], out_ref.at[x], out_sem.at[x]).wait()
    for k in range(len(DIRS)):
        dv, db = DIRS[k]

        @pl.when(there(dv, db))
        def _(k=k):
            copy(k).wait_send()


def convolve_smooth(rect, weights, bias, coef, views, bricks):
    size_x, size_y, ch, depth = rect.shape
    vmem = pl.BlockSpec(memory_space=pltpu.VMEM)
    anyspec = pl.BlockSpec(memory_space=pl.ANY)
    return pl.pallas_call(
        functools.partial(conv_kernel, views, bricks),
        out_shape=jax.ShapeDtypeStruct(rect.shape, jnp.bfloat16),
        in_specs=[anyspec, vmem, vmem, vmem],
        out_specs=anyspec,
        scratch_shapes=[
            pltpu.VMEM((size_x + 4, size_y + 4, ch, depth), jnp.bfloat16),
            pltpu.VMEM(((size_x + 4) * 3 * ch, (size_y + 4) * depth), jnp.bfloat16),
            pltpu.VMEM((3 * ch, (size_y + 4) * depth), jnp.float32),
            pltpu.VMEM((size_x + 2, size_y + 2, ch, depth), jnp.float32),
            pltpu.VMEM((size_x, size_y, ch, depth), jnp.bfloat16),
            pltpu.SemaphoreType.DMA,
            pltpu.SemaphoreType.DMA((len(DIRS),)),
            pltpu.SemaphoreType.DMA((len(DIRS),)),
            pltpu.SemaphoreType.DMA((size_x,)),
        ],
        compiler_params=pltpu.CompilerParams(
            collective_id=0, has_side_effects=True, vmem_limit_bytes=LIMIT
        ),
        name="conv",
    )(rect, weights, bias, coef)


def on_device(
    views, bricks,
    tile_pixel, tile_voxel, tile_count, features, interp, conv_weight, conv_bias, smooth_coef
):
    feats = features[0, 0]
    tiles = interp[0, 0]
    pixel_ids = tile_pixel[0, 0]
    voxel_ids = tile_voxel[0, 0]
    count = tile_count[0, 0]
    slots_total = tiles.shape[0]
    channels = feats.shape[1]
    size_x, size_y, depth = smooth_coef.shape
    per_block = tiles.shape[2] // depth
    blocks = size_x * size_y // per_block
    sender = lax.axis_index("views") * bricks + lax.axis_index("bricks")
    offset = jnp.remainder(sender * 37, slots_total)
    slot_ids = jnp.arange(slots_total, dtype=jnp.int32)
    live = jnp.remainder(slot_ids - offset, slots_total) < count
    ids = jnp.where(live, voxel_ids, blocks)
    partial = lift(pixel_ids, ids, feats, tiles, depth)
    got = lax.all_to_all(partial, ("views", "bricks"), split_axis=0, concat_axis=0, tiled=True)
    got_ids = got[:, got.shape[1] - 8, 0].astype(jnp.int32)
    rect = scatter(got_ids, got, blocks).reshape(size_x, size_y, channels, depth)
    weights = jnp.transpose(conv_weight, (1, 3, 0, 2, 4)).reshape(3 * channels, 9 * channels)
    bias = jnp.broadcast_to(conv_bias[:, None], (channels, depth))
    out = convolve_smooth(rect, weights, bias, smooth_coef, views, bricks)
    return jnp.transpose(out, (2, 0, 1, 3))


def solution(mesh):
    in_specs = (
        P("views", "bricks", None),
        P("views", "bricks", None),
        P("views", "bricks"),
        P("views", "bricks", None, None, None),
        P("views", "bricks", None, None, None),
        P(),
        P(),
        P("bricks", "views", None),
    )
    out_specs = P(None, "bricks", "views", None)
    body = functools.partial(on_device, mesh.shape["views"], mesh.shape["bricks"])
    return jax.shard_map(body, mesh=mesh, in_specs=in_specs, out_specs=out_specs, check_vma=False)
```

```python
import functools

import jax
import jax.numpy as jnp
from jax import lax
from jax.experimental import pallas as pl
from jax.experimental.pallas import tpu as pltpu
from jax.sharding import PartitionSpec as P

MESH = pl.DeviceIdType.MESH
DIRS = ((0, 1), (0, -1), (1, 0), (-1, 0), (1, 1), (1, -1), (-1, 1), (-1, -1))
GROUP = 4
LIMIT = 60 * 1024 * 1024


def lift_kernel(group, pixel_ref, ids_ref, feats_ref, tiles_ref, out_ref):
    step = pl.program_id(0)
    channels = feats_ref.shape[1]
    lanes = out_ref.shape[2]
    parts = tiles_ref.shape[2] // lanes
    for k in range(group):
        slot = step * group + k
        chosen = feats_ref[pixel_ref[slot]]
        value = jnp.dot(chosen, tiles_ref[k], preferred_element_type=jnp.float32)
        value = value.astype(jnp.bfloat16)
        for part in range(parts):
            out_ref[k, part * channels : (part + 1) * channels, :] = value[
                :, part * lanes : (part + 1) * lanes
            ]
        tail = out_ref.shape[1] - parts * channels
        ident = jnp.full((tail, lanes), ids_ref[slot], jnp.int32)
        out_ref[k, parts * channels :, :] = ident.astype(jnp.float32).astype(jnp.bfloat16)


def lift(pixel_ids, ids, feats, tiles, depth):
    slots, pixels, voxels = tiles.shape
    channels = feats.shape[1]
    group = 4
    rows = voxels // depth * channels + 8
    return pl.pallas_call(
        functools.partial(lift_kernel, group),
        out_shape=jax.ShapeDtypeStruct((slots, rows, depth), jnp.bfloat16),
        grid_spec=pltpu.PrefetchScalarGridSpec(
            num_scalar_prefetch=2,
            grid=(slots // group,),
            in_specs=[
                pl.BlockSpec(feats.shape, lambda i, *_: (0, 0, 0)),
                pl.BlockSpec((group, pixels, voxels), lambda i, *_: (i, 0, 0)),
            ],
            out_specs=pl.BlockSpec((group, rows, depth), lambda i, *_: (i, 0, 0)),
        ),
        name="lift",
    )(pixel_ids, ids, feats, tiles)


def scatter_kernel(ids_ref, got_ref, out_ref, acc):
    slots = got_ref.shape[0]
    blocks = out_ref.shape[0]
    rows = out_ref.shape[1]

    def clear(i, _):
        acc[i] = jnp.zeros(acc.shape[1:], jnp.float32)
        return 0

    def add(d, _):
        i = ids_ref[d]
        acc[i] = acc[i] + got_ref[d, 0:rows, :].astype(jnp.float32)
        return 0

    def put(i, _):
        out_ref[i] = jnp.maximum(acc[i], 0.0).astype(jnp.bfloat16)
        return 0

    lax.fori_loop(0, blocks, clear, 0)
    lax.fori_loop(0, slots, add, 0)
    lax.fori_loop(0, blocks, put, 0)


def scatter(ids, got, blocks):
    rows = got.shape[1] - 8
    depth = got.shape[2]
    return pl.pallas_call(
        scatter_kernel,
        out_shape=jax.ShapeDtypeStruct((blocks, rows, depth), jnp.bfloat16),
        grid_spec=pltpu.PrefetchScalarGridSpec(
            num_scalar_prefetch=1,
            grid=(1,),
            in_specs=[pl.BlockSpec(got.shape, lambda i, *_: (0, 0, 0))],
            out_specs=pl.BlockSpec((blocks, rows, depth), lambda i, *_: (0, 0, 0)),
            scratch_shapes=[pltpu.VMEM((blocks + 1, rows, depth), jnp.float32)],
        ),
        compiler_params=pltpu.CompilerParams(vmem_limit_bytes=LIMIT),
        name="scatter",
    )(ids, got)


def conv_kernel(
    views, bricks, r_ref, w_ref, bias_ref, coef_ref, out_ref,
    padded, prod, gated, obuf, own_sem, send_sem, recv_sem, out_sem,
):
    v = lax.axis_index("views")
    b = lax.axis_index("bricks")
    size_x, size_y, ch, depth = r_ref.shape
    wide = 3 * ch

    def there(dv, db):
        return (v + dv >= 0) & (v + dv < views) & (b + db >= 0) & (b + db < bricks)

    def count(dv, db):
        return jnp.where(there(dv, db), 1, 0)

    own = pltpu.make_async_copy(
        r_ref, padded.at[pl.ds(2, size_x), pl.ds(2, size_y)], own_sem
    )
    own.start()

    barrier = pltpu.get_barrier_semaphore()
    total = 0
    for dv, db in DIRS:
        total = total + count(dv, db)

        @pl.when(there(dv, db))
        def _(dv=dv, db=db):
            pl.semaphore_signal(barrier, inc=1, device_id=(v + dv, b + db), device_id_type=MESH)

    pl.semaphore_wait(barrier, total)

    def span(delta, size):
        if delta == 0:
            return pl.ds(0, size), pl.ds(2, size)
        if delta == 1:
            return pl.ds(size - 2, 2), pl.ds(0, 2)
        return pl.ds(0, 2), pl.ds(size + 2, 2)

    def copy(k):
        dv, db = DIRS[k]
        from_x, to_x = span(db, size_x)
        from_y, to_y = span(dv, size_y)
        return pltpu.make_async_remote_copy(
            src_ref=r_ref.at[from_x, from_y],
            dst_ref=padded.at[to_x, to_y],
            send_sem=send_sem.at[k],
            recv_sem=recv_sem.at[k],
            device_id=(v + dv, b + db),
            device_id_type=MESH,
        )

    for k in range(len(DIRS)):
        dv, db = DIRS[k]

        @pl.when(there(dv, db))
        def _(k=k):
            copy(k).start()

    def receive(k):
        dv, db = DIRS[k]
        _, to_x = span(db, size_x)
        _, to_y = span(dv, size_y)

        @pl.when(there(-dv, -db))
        def _():
            copy(k).wait_recv()

        @pl.when(jnp.logical_not(there(-dv, -db)))
        def _():
            view = padded.at[to_x, to_y]
            view[...] = jnp.zeros(view.shape, jnp.bfloat16)

    lane = lax.broadcasted_iota(jnp.int32, (ch, depth), 1)

    def beside_z(low, high):
        before = jnp.where(lane == 0, 0.0, pltpu.roll(low, 1, 1))
        after = jnp.where(lane == depth - 1, 0.0, pltpu.roll(high, depth - 1, 1))
        return before + after

    def start_rows(slot, g, y):
        tall = [
            jnp.concatenate([padded[g + dx, y + dy + j] for j in range(GROUP)], axis=1)
            for dx in range(3)
            for dy in range(3)
        ]
        prod[slot] = jnp.dot(
            w_ref[...], jnp.concatenate(tall, axis=0), preferred_element_type=jnp.float32
        )

    def finish_rows(slot, g, y):
        x_all = b * size_x + g - 1
        x_fits = (x_all >= 0) & (x_all < bricks * size_x)
        for j in range(GROUP):
            at = slice(j * depth, (j + 1) * depth)
            value = prod[slot, ch : 2 * ch, at]
            value = value + beside_z(prod[slot, 0:ch, at], prod[slot, 2 * ch : wide, at])
            value = jnp.maximum(value + bias_ref[...], 0.0)
            y_all = v * size_y + y + j - 1
            fits = x_fits & (y_all >= 0) & (y_all < views * size_y)
            gated[g, y + j] = value * jnp.where(fits, 1.0, 0.0)

    def loop(low, high, body, unroll=1):
        def step(i, _):
            body(i)
            return 0

        lax.fori_loop(low, high, step, 0, unroll=unroll)

    groups = size_y // GROUP

    def smooth_rows(x, y):
        here = gated[x + 1, y + 1]
        beside = gated[x, y + 1] + gated[x + 2, y + 1] + gated[x + 1, y] + gated[x + 1, y + 2]
        beside = beside + beside_z(here, here)
        coef = coef_ref[x, pl.ds(y, 1), :]
        obuf[x, y] = (here + coef * (beside - 6.0 * here)).astype(jnp.bfloat16)

    def put(x):
        pltpu.make_async_copy(obuf.at[x], out_ref.at[x], out_sem.at[x]).start()

    def run_rows(g, starts, x=None):
        for i, y in enumerate(starts):
            start_rows(i % 2, g, y)
            if x is not None:
                for j in range(GROUP):
                    if i * GROUP + j < size_y:
                        smooth_rows(x, i * GROUP + j)
            if i:
                finish_rows((i - 1) % 2, g, starts[i - 1])
        finish_rows((len(starts) - 1) % 2, g, starts[-1])
        if x is not None:
            put(x)

    def loop(low, high, body):
        def step(i, _):
            body(i)
            return 0

        lax.fori_loop(low, high, step, 0)

    middle = [GROUP * c for c in range(1, size_y // GROUP)]
    ends = [0, size_y + 2 - GROUP]
    rows = [0] + middle + [size_y + 2 - GROUP]

    own.wait()
    loop(2, 5, lambda g: run_rows(g, middle))
    receive(2)
    receive(3)
    loop(2, 5, lambda g: run_rows(g, ends))
    loop(5, size_x, lambda g: run_rows(g, rows, g - 3))
    for k in (0, 1, 4, 5, 6, 7):
        receive(k)
    loop(size_x, size_x + 2, lambda g: run_rows(g, rows, g - 3))
    loop(0, 2, lambda i: run_rows(1 - i, rows, jnp.where(i == 0, size_x - 1, 1)))

    def first(y):
        for j in range(GROUP):
            smooth_rows(0, y * GROUP + j)

    loop(0, size_y // GROUP, first)
    put(0)
    for x in range(size_x):
        pltpu.make_async_copy(obuf.at[x], out_ref.at[x], out_sem.at[x]).wait()
    for k in range(len(DIRS)):
        dv, db = DIRS[k]

        @pl.when(there(dv, db))
        def _(k=k):
            copy(k).wait_send()


def convolve_smooth(rect, weights, bias, coef, views, bricks):
    size_x, size_y, ch, depth = rect.shape
    vmem = pl.BlockSpec(memory_space=pltpu.VMEM)
    anyspec = pl.BlockSpec(memory_space=pl.ANY)
    return pl.pallas_call(
        functools.partial(conv_kernel, views, bricks),
        out_shape=jax.ShapeDtypeStruct(rect.shape, jnp.bfloat16),
        in_specs=[anyspec, vmem, vmem, vmem],
        out_specs=anyspec,
        scratch_shapes=[
            pltpu.VMEM((size_x + 4, size_y + 4, ch, depth), jnp.bfloat16),
            pltpu.VMEM((2, 3 * ch, GROUP * depth), jnp.float32),
            pltpu.VMEM((size_x + 2, size_y + 2, ch, depth), jnp.float32),
            pltpu.VMEM((size_x, size_y, ch, depth), jnp.bfloat16),
            pltpu.SemaphoreType.DMA,
            pltpu.SemaphoreType.DMA((len(DIRS),)),
            pltpu.SemaphoreType.DMA((len(DIRS),)),
            pltpu.SemaphoreType.DMA((size_x,)),
        ],
        compiler_params=pltpu.CompilerParams(
            collective_id=0, has_side_effects=True, vmem_limit_bytes=LIMIT
        ),
        name="conv",
    )(rect, weights, bias, coef)


def on_device(
    views, bricks,
    tile_pixel, tile_voxel, tile_count, features, interp, conv_weight, conv_bias, smooth_coef
):
    feats = features[0, 0]
    tiles = interp[0, 0]
    pixel_ids = tile_pixel[0, 0]
    voxel_ids = tile_voxel[0, 0]
    count = tile_count[0, 0]
    slots_total = tiles.shape[0]
    channels = feats.shape[1]
    size_x, size_y, depth = smooth_coef.shape
    per_block = tiles.shape[2] // depth
    blocks = size_x * size_y // per_block
    sender = lax.axis_index("views") * bricks + lax.axis_index("bricks")
    offset = jnp.remainder(sender * 37, slots_total)
    slot_ids = jnp.arange(slots_total, dtype=jnp.int32)
    live = jnp.remainder(slot_ids - offset, slots_total) < count
    ids = jnp.where(live, voxel_ids, blocks)
    partial = lift(pixel_ids, ids, feats, tiles, depth)
    got = lax.all_to_all(partial, ("views", "bricks"), split_axis=0, concat_axis=0, tiled=True)
    got_ids = got[:, got.shape[1] - 8, 0].astype(jnp.int32)
    rect = scatter(got_ids, got, blocks).reshape(size_x, size_y, channels, depth)
    weights = jnp.transpose(conv_weight, (2, 3, 0, 1, 4)).reshape(3 * channels, 9 * channels)
    bias = jnp.broadcast_to(conv_bias[:, None], (channels, depth))
    out = convolve_smooth(rect, weights, bias, smooth_coef, views, bricks)
    return jnp.transpose(out, (2, 0, 1, 3))


def solution(mesh):
    in_specs = (
        P("views", "bricks", None),
        P("views", "bricks", None),
        P("views", "bricks"),
        P("views", "bricks", None, None, None),
        P("views", "bricks", None, None, None),
        P(),
        P(),
        P("bricks", "views", None),
    )
    out_specs = P(None, "bricks", "views", None)
    body = functools.partial(on_device, mesh.shape["views"], mesh.shape["bricks"])
    return jax.shard_map(body, mesh=mesh, in_specs=in_specs, out_specs=out_specs, check_vma=False)
```

```python
import functools

import jax
import jax.numpy as jnp
from jax import lax
from jax.experimental import pallas as pl
from jax.experimental.pallas import tpu as pltpu
from jax.sharding import PartitionSpec as P

MESH = pl.DeviceIdType.MESH
DIRS = ((0, 1), (0, -1), (1, 0), (-1, 0), (1, 1), (1, -1), (-1, 1), (-1, -1))
SENDS = (
    (0, 1, 0), (0, -1, 0), (1, 0, None), (-1, 0, None),
    (1, 1, None), (1, -1, None), (-1, 1, None), (-1, -1, None),
    (0, 1, 1), (0, -1, 1),
)
GROUP = 4
LIMIT = 60 * 1024 * 1024


def lift_kernel(pixel_ref, ids_ref, feats_ref, *refs):
    streams, out_ref = refs[:-1], refs[-1]
    each = streams[0].shape[0]
    group = each * len(streams)
    step = pl.program_id(0)
    channels = feats_ref.shape[1]
    lanes = out_ref.shape[2]
    parts = streams[0].shape[2] // lanes
    for k in range(group):
        slot = step * group + k
        chosen = feats_ref[pixel_ref[slot]]
        value = jnp.dot(chosen, streams[k // each][k % each], preferred_element_type=jnp.float32)
        value = value.astype(jnp.bfloat16)
        for part in range(parts):
            out_ref[k, part * channels : (part + 1) * channels, :] = value[
                :, part * lanes : (part + 1) * lanes
            ]
        tail = out_ref.shape[1] - parts * channels
        ident = jnp.full((tail, lanes), ids_ref[slot], jnp.int32)
        out_ref[k, parts * channels :, :] = ident.astype(jnp.float32).astype(jnp.bfloat16)


def lift(pixel_ids, ids, feats, tiles, depth):
    slots, pixels, voxels = tiles.shape
    channels = feats.shape[1]
    streams, each = 4, 2
    group = streams * each
    rows = voxels // depth * channels + 8
    return pl.pallas_call(
        lift_kernel,
        out_shape=jax.ShapeDtypeStruct((slots, rows, depth), jnp.bfloat16),
        grid_spec=pltpu.PrefetchScalarGridSpec(
            num_scalar_prefetch=2,
            grid=(slots // group,),
            in_specs=[
                pl.BlockSpec(feats.shape, lambda i, *_: (0, 0, 0)),
            ]
            + [
                pl.BlockSpec((each, pixels, voxels), lambda i, *_, q=q: (i * streams + q, 0, 0))
                for q in range(streams)
            ],
            out_specs=pl.BlockSpec((group, rows, depth), lambda i, *_: (i, 0, 0)),
        ),
        name="lift",
    )(pixel_ids, ids, feats, *[tiles] * streams)


def scatter_kernel(ids_ref, got_ref, out_ref, acc):
    slots = got_ref.shape[0]
    blocks = out_ref.shape[0]
    rows = out_ref.shape[1]

    def clear(i, _):
        acc[i] = jnp.zeros(acc.shape[1:], jnp.float32)
        return 0

    def add(d, _):
        i = ids_ref[d]
        acc[i] = acc[i] + got_ref[d, 0:rows, :].astype(jnp.float32)
        return 0

    def put(i, _):
        out_ref[i] = jnp.maximum(acc[i], 0.0).astype(jnp.bfloat16)
        return 0

    lax.fori_loop(0, blocks, clear, 0)
    lax.fori_loop(0, slots, add, 0)
    lax.fori_loop(0, blocks, put, 0)


def scatter(ids, got, blocks):
    rows = got.shape[1] - 8
    depth = got.shape[2]
    return pl.pallas_call(
        scatter_kernel,
        out_shape=jax.ShapeDtypeStruct((blocks, rows, depth), jnp.bfloat16),
        grid_spec=pltpu.PrefetchScalarGridSpec(
            num_scalar_prefetch=1,
            grid=(1,),
            in_specs=[pl.BlockSpec(got.shape, lambda i, *_: (0, 0, 0))],
            out_specs=pl.BlockSpec((blocks, rows, depth), lambda i, *_: (0, 0, 0)),
            scratch_shapes=[pltpu.VMEM((blocks + 1, rows, depth), jnp.float32)],
        ),
        compiler_params=pltpu.CompilerParams(vmem_limit_bytes=LIMIT),
        name="scatter",
    )(ids, got)


def conv_kernel(
    views, bricks, r_ref, w_ref, bias_ref, coef_ref, out_ref,
    padded, prod, gated, obuf, own_sem, send_sem, recv_sem, out_sem,
):
    v = lax.axis_index("views")
    b = lax.axis_index("bricks")
    size_x, size_y, ch, depth = r_ref.shape
    wide = 3 * ch

    def there(dv, db):
        return (v + dv >= 0) & (v + dv < views) & (b + db >= 0) & (b + db < bricks)

    def count(dv, db):
        return jnp.where(there(dv, db), 1, 0)

    own = pltpu.make_async_copy(
        r_ref, padded.at[pl.ds(2, size_x), pl.ds(2, size_y)], own_sem
    )
    own.start()

    barrier = pltpu.get_barrier_semaphore()
    total = 0
    for dv, db in DIRS:
        total = total + count(dv, db)

        @pl.when(there(dv, db))
        def _(dv=dv, db=db):
            pl.semaphore_signal(barrier, inc=1, device_id=(v + dv, b + db), device_id_type=MESH)

    pl.semaphore_wait(barrier, total)

    def span(delta, size, plane=None):
        if delta == 0:
            return pl.ds(0, size), pl.ds(2, size)
        if plane is None:
            low, width = 0, 2
        else:
            low, width = (1 - plane if delta == 1 else plane), 1
        if delta == 1:
            return pl.ds(size - 2 + low, width), pl.ds(low, width)
        return pl.ds(low, width), pl.ds(size + 2 + low, width)

    def copy(k):
        dv, db, plane = SENDS[k]
        from_x, to_x = span(db, size_x, plane)
        from_y, to_y = span(dv, size_y)
        return pltpu.make_async_remote_copy(
            src_ref=r_ref.at[from_x, from_y],
            dst_ref=padded.at[to_x, to_y],
            send_sem=send_sem.at[k],
            recv_sem=recv_sem.at[k],
            device_id=(v + dv, b + db),
            device_id_type=MESH,
        )

    for k, (dv, db, _) in enumerate(SENDS):

        @pl.when(there(dv, db))
        def _(k=k):
            copy(k).start()

    def receive(k):
        dv, db, plane = SENDS[k]
        _, to_x = span(db, size_x, plane)
        _, to_y = span(dv, size_y)

        @pl.when(there(-dv, -db))
        def _():
            copy(k).wait_recv()

        @pl.when(jnp.logical_not(there(-dv, -db)))
        def _():
            view = padded.at[to_x, to_y]
            view[...] = jnp.zeros(view.shape, jnp.bfloat16)

    lane = lax.broadcasted_iota(jnp.int32, (ch, depth), 1)

    def beside_z(low, high):
        before = jnp.where(lane == 0, 0.0, pltpu.roll(low, 1, 1))
        after = jnp.where(lane == depth - 1, 0.0, pltpu.roll(high, depth - 1, 1))
        return before + after

    def start_rows(slot, g, y):
        tall = [
            jnp.concatenate([padded[g + dx, y + dy + j] for j in range(GROUP)], axis=1)
            for dx in range(3)
            for dy in range(3)
        ]
        prod[slot] = jnp.dot(
            w_ref[...], jnp.concatenate(tall, axis=0), preferred_element_type=jnp.float32
        )

    def finish_rows(slot, g, y):
        x_all = b * size_x + g - 1
        x_fits = (x_all >= 0) & (x_all < bricks * size_x)
        for j in range(GROUP):
            at = slice(j * depth, (j + 1) * depth)
            value = prod[slot, ch : 2 * ch, at]
            value = value + beside_z(prod[slot, 0:ch, at], prod[slot, 2 * ch : wide, at])
            value = jnp.maximum(value + bias_ref[...], 0.0)
            y_all = v * size_y + y + j - 1
            fits = x_fits & (y_all >= 0) & (y_all < views * size_y)
            gated[g, y + j] = value * jnp.where(fits, 1.0, 0.0)

    def loop(low, high, body, unroll=1):
        def step(i, _):
            body(i)
            return 0

        lax.fori_loop(low, high, step, 0, unroll=unroll)

    groups = size_y // GROUP

    def smooth_rows(x, y):
        here = gated[x + 1, y + 1]
        beside = gated[x, y + 1] + gated[x + 2, y + 1] + gated[x + 1, y] + gated[x + 1, y + 2]
        beside = beside + beside_z(here, here)
        coef = coef_ref[x, pl.ds(y, 1), :]
        obuf[x, y] = (here + coef * (beside - 6.0 * here)).astype(jnp.bfloat16)

    def put(x):
        pltpu.make_async_copy(obuf.at[x], out_ref.at[x], out_sem.at[x]).start()

    def run_rows(g, starts, x=None):
        for i, y in enumerate(starts):
            start_rows(i % 2, g, y)
            if x is not None:
                for j in range(GROUP):
                    if i * GROUP + j < size_y:
                        smooth_rows(x, i * GROUP + j)
            if i:
                finish_rows((i - 1) % 2, g, starts[i - 1])
        finish_rows((len(starts) - 1) % 2, g, starts[-1])
        if x is not None:
            put(x)

    def loop(low, high, body):
        def step(i, _):
            body(i)
            return 0

        lax.fori_loop(low, high, step, 0)

    middle = [GROUP * c for c in range(1, size_y // GROUP)]
    ends = [0, size_y + 2 - GROUP]
    rows = [0] + middle + [size_y + 2 - GROUP]

    own.wait()
    loop(2, 5, lambda g: run_rows(g, middle))
    receive(2)
    receive(3)
    loop(2, 5, lambda g: run_rows(g, ends))
    loop(5, size_x, lambda g: run_rows(g, rows, g - 3))
    low_first = b < bricks // 2

    def boundary(i):
        low_side = (i < 2) == low_first
        odd = lax.rem(i, 2)
        for db, side in ((1, low_side), (-1, jnp.logical_not(low_side))):
            for plane in range(2):
                keys = [
                    k
                    for k, (dv, step, part) in enumerate(SENDS)
                    if step == db and (part == plane or (part is None and plane == 0))
                ]

                @pl.when(side & (odd == plane))
                def _(keys=keys):
                    for k in keys:
                        receive(k)

        g = jnp.where(low_side, 1 - odd, size_x + odd)
        ahead = jnp.where(i == 1, 1, jnp.where(i == 2, 0, size_x - 2))
        behind = jnp.where(i == 1, size_x - 2, jnp.where(i == 2, size_x - 1, 1))
        x = jnp.where(i == 0, size_x - 3, jnp.where(low_first, ahead, behind))
        run_rows(g, rows, x)

    loop(0, 4, boundary)
    last = jnp.where(low_first, size_x - 1, 0)

    def finish(y):
        for j in range(GROUP):
            smooth_rows(last, y * GROUP + j)

    loop(0, size_y // GROUP, finish)
    put(last)
    for x in range(size_x):
        pltpu.make_async_copy(obuf.at[x], out_ref.at[x], out_sem.at[x]).wait()
    for k, (dv, db, _) in enumerate(SENDS):

        @pl.when(there(dv, db))
        def _(k=k):
            copy(k).wait_send()


def convolve_smooth(rect, weights, bias, coef, views, bricks):
    size_x, size_y, ch, depth = rect.shape
    vmem = pl.BlockSpec(memory_space=pltpu.VMEM)
    anyspec = pl.BlockSpec(memory_space=pl.ANY)
    return pl.pallas_call(
        functools.partial(conv_kernel, views, bricks),
        out_shape=jax.ShapeDtypeStruct(rect.shape, jnp.bfloat16),
        in_specs=[anyspec, vmem, vmem, vmem],
        out_specs=anyspec,
        scratch_shapes=[
            pltpu.VMEM((size_x + 4, size_y + 4, ch, depth), jnp.bfloat16),
            pltpu.VMEM((2, 3 * ch, GROUP * depth), jnp.float32),
            pltpu.VMEM((size_x + 2, size_y + 2, ch, depth), jnp.float32),
            pltpu.VMEM((size_x, size_y, ch, depth), jnp.bfloat16),
            pltpu.SemaphoreType.DMA,
            pltpu.SemaphoreType.DMA((len(SENDS),)),
            pltpu.SemaphoreType.DMA((len(SENDS),)),
            pltpu.SemaphoreType.DMA((size_x,)),
        ],
        compiler_params=pltpu.CompilerParams(
            collective_id=0, has_side_effects=True, vmem_limit_bytes=LIMIT
        ),
        name="conv",
    )(rect, weights, bias, coef)


def on_device(
    views, bricks,
    tile_pixel, tile_voxel, tile_count, features, interp, conv_weight, conv_bias, smooth_coef
):
    feats = features[0, 0]
    tiles = interp[0, 0]
    pixel_ids = tile_pixel[0, 0]
    voxel_ids = tile_voxel[0, 0]
    count = tile_count[0, 0]
    slots_total = tiles.shape[0]
    channels = feats.shape[1]
    size_x, size_y, depth = smooth_coef.shape
    per_block = tiles.shape[2] // depth
    blocks = size_x * size_y // per_block
    sender = lax.axis_index("views") * bricks + lax.axis_index("bricks")
    offset = jnp.remainder(sender * 37, slots_total)
    slot_ids = jnp.arange(slots_total, dtype=jnp.int32)
    live = jnp.remainder(slot_ids - offset, slots_total) < count
    ids = jnp.where(live, voxel_ids, blocks)
    partial = lift(pixel_ids, ids, feats, tiles, depth)
    got = lax.all_to_all(partial, ("views", "bricks"), split_axis=0, concat_axis=0, tiled=True)
    got_ids = got[:, got.shape[1] - 8, 0].astype(jnp.int32)
    rect = scatter(got_ids, got, blocks).reshape(size_x, size_y, channels, depth)
    weights = jnp.transpose(conv_weight, (2, 3, 0, 1, 4)).reshape(3 * channels, 9 * channels)
    bias = jnp.broadcast_to(conv_bias[:, None], (channels, depth))
    out = convolve_smooth(rect, weights, bias, smooth_coef, views, bricks)
    return jnp.transpose(out, (2, 0, 1, 3))


def solution(mesh):
    in_specs = (
        P("views", "bricks", None),
        P("views", "bricks", None),
        P("views", "bricks"),
        P("views", "bricks", None, None, None),
        P("views", "bricks", None, None, None),
        P(),
        P(),
        P("bricks", "views", None),
    )
    out_specs = P(None, "bricks", "views", None)
    body = functools.partial(on_device, mesh.shape["views"], mesh.shape["bricks"])
    return jax.shard_map(body, mesh=mesh, in_specs=in_specs, out_specs=out_specs, check_vma=False)
```
